512 devices in a mesh: seq: 32 (over y, x), head: 16 (over z, core).
Axes of the slice: x: 4, y: 8, z: 8, core: 2. Of those that a mesh axis runs over, the one named last changes fastest.
Arguments:
- inputs: bfloat16 [16384, 4096], P('seq', 'head'), may hold values from -6 to 6
- gate: bfloat16 [16384, 4096], P('seq', 'head'), may hold values from -6 to 6
- input_map: bfloat16 [128, 16384], P('head', 'seq'), may hold values from -3 to 3
- output_map: bfloat16 [128, 16384], P('head', 'seq'), may hold values from -3 to 3
- step: float32 [64, 16384], P('head', 'seq'), may hold values from 0.25 to 2
- decay_rate: float32 [64], P('head'), may hold values from 3e-05 to 0.03
- level_mix: float32 [9, 64, 16384], P(None, 'head', 'seq'), may hold values from 0.1 to 1
- skip: float32 [64], P('head'), may hold values from 0.25 to 0.75
- norm_gain: float32 [4096], P('head'), may hold values from 0.5 to 1.5
Outputs:
- normed: bfloat16 [16384, 4096], P('seq', 'head')
The draws below stay inside these ranges and needn't reach their ends.
All inputs are finite; a program needn't handle non-finite values.
Results may differ from the reference program's by a relative error of at most 0.0075.
Values may be sent and summed in bfloat16 or wider, within the bound.
A program may use at most 64 MiB of HBM per device.

```python
import math
import jax
import jax.numpy as jnp
from jax import lax

HEADS = 64
P_SIZE = 64
N = 128
GROUP = 256
LEVELS = 9
TOKENS = 16384


def block_levels(own_key, extent, cuts, smallest, largest):
    loudness = 1.0
    for dim, blocks in cuts:
        steps = jax.random.uniform(jax.random.fold_in(jax.random.fold_in(own_key, 6), dim), (blocks,), jnp.float32, smallest / len(cuts), largest / len(cuts))
        loudness = loudness * jnp.repeat(jnp.exp(steps), extent[dim] // blocks).reshape((-1,) + (1,) * (len(extent) - 1 - dim))
    return loudness


def gaussian(stream_key, shape, width, reach, cuts=(), kind=jnp.bfloat16):
    drawn = jax.random.normal(stream_key, shape, jnp.float32) * width
    if len(cuts) > 0:
        drawn = block_levels(stream_key, shape, cuts, -0.22, 0.18) * drawn
    return jnp.clip(drawn, min=-reach, max=reach).astype(kind)


def setup_inputs(seed: int = 0) -> dict:
    streams_of = jax.random.split(jax.random.key(seed), 10)
    inputs = gaussian(streams_of[0], (TOKENS, HEADS * P_SIZE), 1.0, 6.0, ((0, 32), (1, 16)))
    gate = gaussian(streams_of[1], (TOKENS, HEADS * P_SIZE), 1.0, 6.0, ((0, 32), (1, 16)))
    input_map = gaussian(streams_of[2], (N, TOKENS), 0.5, 3.0, ((0, 16), (1, 32)))
    output_map = gaussian(streams_of[3], (N, TOKENS), 0.5, 3.0, ((0, 16), (1, 32)))
    step = jnp.clip(jnp.exp(math.log(2.0) - 2.0794415 * jax.random.uniform(streams_of[4], (HEADS, TOKENS), jnp.float32) ** block_levels(streams_of[4], (HEADS, TOKENS), ((0, 16), (1, 32)), -0.2, 0.2)), 0.25, 2.0)
    decay_rate = jnp.clip(jnp.exp(math.log(0.03) - 6.9077553 * jax.random.uniform(streams_of[5], (HEADS,), jnp.float32) ** block_levels(streams_of[5], (HEADS,), ((0, 16),), -0.2, 0.2)), 2.9999999242136255e-05, 0.03)
    level_mix = jnp.clip(0.1 + 0.9 * jax.random.uniform(streams_of[6], (LEVELS, HEADS, TOKENS), jnp.float32) ** block_levels(streams_of[6], (LEVELS, HEADS, TOKENS), ((1, 16), (2, 32)), -0.2, 0.2), 0.1, 1.0)
    skip = jnp.clip(0.25 + 0.5 * jax.random.uniform(streams_of[7], (HEADS,), jnp.float32) ** block_levels(streams_of[7], (HEADS,), ((0, 16),), -0.2, 0.2), 0.25, 0.75)
    norm_gain = jnp.clip(1.0 + 0.1 * jax.random.normal(streams_of[8], (HEADS * P_SIZE,), jnp.float32), 0.5, 1.5)
    return dict(inputs=inputs, gate=gate, input_map=input_map, output_map=output_map, step=step, decay_rate=decay_rate, level_mix=level_mix, skip=skip, norm_gain=norm_gain)


def reference(inputs, gate, input_map, output_map, step, decay_rate, level_mix, skip, norm_gain):
    groups = TOKENS // GROUP
    spans = LEVELS - 1
    highest = lax.Precision.HIGHEST
    pieces = (inputs.reshape(groups, GROUP, HEADS, P_SIZE), gate.reshape(groups, GROUP, HEADS * P_SIZE), input_map.reshape(N, groups, GROUP).transpose(1, 0, 2), output_map.reshape(N, groups, GROUP).transpose(1, 0, 2), step.reshape(HEADS, groups, GROUP).transpose(1, 0, 2), level_mix.reshape(LEVELS, HEADS, groups, GROUP).transpose(2, 0, 1, 3), jnp.arange(groups, dtype=jnp.int32))
    powers = jnp.left_shift(jnp.int32(1), jnp.arange(spans, dtype=jnp.int32))
    rows = jnp.arange(GROUP, dtype=jnp.int32)
    causal = rows[:, None] >= rows[None, :]

    def advance(carry, piece):
        values, gates, in_c, out_c, step_c, mix_c, index = piece
        cum = jnp.cumsum(-step_c * decay_rate[:, None], axis=1)
        scores = jnp.dot(out_c.T, in_c, preferred_element_type=jnp.float32)
        spread = cum[:, :, None] - cum[:, None, :]
        within = jnp.where(causal[None], jnp.exp(jnp.where(causal[None], spread, 0.0)), 0.0)
        weights = (scores[None] * within * step_c[:, None, :]).astype(jnp.bfloat16)
        v32 = values.astype(jnp.float32)
        intra = jnp.einsum('hts,shp->thp', weights.astype(jnp.float32), v32, precision=highest)
        proj = jnp.einsum('nt,bhnp->bthp', out_c.astype(jnp.float32), carry, precision=highest)
        spanned = jnp.einsum('bht,bthp->thp', mix_c[1:], proj, precision=highest)
        spanned = spanned * jnp.exp(cum).T[:, :, None]
        y = mix_c[0].T[:, :, None] * intra + spanned + skip[None, :, None] * v32
        gated = y.reshape(GROUP, HEADS * P_SIZE) * jax.nn.silu(gates.astype(jnp.float32))
        scale = lax.rsqrt(lax.optimization_barrier(jnp.mean(gated * gated, axis=1, keepdims=True)) + 1e-05)
        out = (gated * scale * norm_gain[None, :]).astype(jnp.bfloat16)
        loads = (in_c[None] * (jnp.exp(cum[:, -1:] - cum) * step_c)[:, None, :]).astype(jnp.bfloat16)
        state = jnp.einsum('hns,shp->hnp', loads.astype(jnp.float32), v32, precision=highest)
        decay = jnp.exp(cum[:, -1])[None, :, None, None]
        flag = jnp.bitwise_and(index + 1, jnp.bitwise_not(index))
        hit = (powers == flag)[:, None, None, None]
        low = (powers < flag)[:, None, None, None]
        merged = decay[0] * lax.optimization_barrier(jnp.sum(jnp.where(low, carry, 0.0), axis=0)) + state
        fresh = jnp.where(hit, merged[None], jnp.where(low, 0.0, decay * carry))
        return (fresh, out)
    start = jnp.zeros((spans, HEADS, N, P_SIZE), jnp.float32)
    _, outs = lax.scan(advance, start, pieces)
    return outs.reshape(TOKENS, HEADS * P_SIZE)
```

```python
import functools

import jax
import jax.numpy as jnp
from jax import lax
from jax.experimental import pallas as pl
from jax.experimental.pallas import tpu as pltpu
from jax.sharding import PartitionSpec as P

P_SIZE = 64
N = 128
GROUP = 256
EPS = 1e-05
X = 4
F32, BF16 = jnp.float32, jnp.bfloat16
MESH = pl.DeviceIdType.MESH


def ring_offsets(chips):
    order = []
    for far in range(chips // 2, 0, -1):
        ways = (far,) if 2 * far == chips else (far, chips - far)
        order += [(way, flip) for flip in (0, 1) for way in ways]
    return order + [(0, 1)]


def iota(shape, dim):
    return lax.broadcasted_iota(jnp.int32, shape, dim)


def dot(a, b):
    return jnp.dot(a, b, preferred_element_type=F32)


def split_rows(v):
    high = v.astype(BF16).astype(F32)
    return jnp.where(iota(v.shape, 0) < 4, high, v - high)


def lanes(tile):
    low = iota((1, 128), 1) < P_SIZE
    return jnp.concatenate(
        [jnp.where(low, tile[0:1], tile[1:2]), jnp.where(low, tile[2:3], tile[3:4])], axis=1
    )


def kernel(
    rows_y, chips_z,
    x_hbm, gate_hbm, b_ref, c_ref, step_ref, rate_ref, mix_hbm, skip_ref, gain_ref,
    out_ref,
    x_ref, gate_ref, mix_ref, b_all, c_all, drive, factor, silu, pre, gated, ct_ref,
    state, piece, row_state, tot, row_tot, row_sum, row_in, span, squares,
    near_state,
    local_sem, z_send, z_recv, x_send, x_recv, y_send, y_recv,
):
    shard, col = lax.axis_index("seq"), lax.axis_index("head")
    y, x = shard // X, shard % X
    z, core = col // 2, col % 2
    heads = 2 * chips_z
    own = b_ref.shape[0]
    cut = N // X
    bits_y = rows_y.bit_length() - 1
    offsets = ring_offsets(chips_z)

    def z_peer(offset):
        way, flip = offset
        return ((z + way) % chips_z) * 2 + (core + flip) % 2

    def z_copy(kind, slot, src, dst):
        return pltpu.make_async_remote_copy(
            src_ref=src, dst_ref=dst, send_sem=z_send.at[kind, slot], recv_sem=z_recv.at[kind, slot],
            device_id=(shard, z_peer(offsets[slot])), device_id_type=MESH,
        )

    def x_copy(kind, ahead, src, dst):
        return pltpu.make_async_remote_copy(
            src_ref=src, dst_ref=dst, send_sem=x_send.at[kind, ahead], recv_sem=x_recv.at[kind, ahead],
            device_id=(y * X + (x + ahead) % X, col), device_id_type=MESH,
        )

    def y_copy(kind, ahead, src, dst):
        return pltpu.make_async_remote_copy(
            src_ref=src, dst_ref=dst, send_sem=y_send.at[kind, ahead], recv_sem=y_recv.at[kind, ahead],
            device_id=(((y + ahead) % rows_y) * X + x, col), device_id_type=MESH,
        )

    barrier = pltpu.get_barrier_semaphore()
    for offset in offsets:
        pl.semaphore_signal(barrier, inc=1, device_id=(shard, z_peer(offset)), device_id_type=MESH)
    for ahead in range(1, X):
        pl.semaphore_signal(
            barrier, inc=1, device_id=(y * X + (x + ahead) % X, col), device_id_type=MESH
        )
    for ahead in range(1, rows_y):
        pl.semaphore_signal(
            barrier, inc=1, device_id=(((y + ahead) % rows_y) * X + x, col), device_id_type=MESH
        )

    mine = pl.ds(pl.multiple_of(col * own, own), own)
    loads = [
        pltpu.make_async_copy(x_hbm, x_ref, local_sem.at[0]),
        pltpu.make_async_copy(mix_hbm, mix_ref, local_sem.at[1]),
        pltpu.make_async_copy(gate_hbm, gate_ref, local_sem.at[2]),
        pltpu.make_async_copy(b_ref, b_all.at[mine], local_sem.at[3]),
        pltpu.make_async_copy(c_ref, c_all.at[mine], local_sem.at[4]),
    ]
    for load in loads:
        load.start()

    rate = jnp.zeros((8, 1), F32)
    skip = jnp.zeros((1, 256), F32)
    for head in range(4):
        rate = jnp.where(iota((8, 1), 0) % 4 == head, rate_ref[head], rate)
        skip = jnp.where(iota((1, 256), 1) // P_SIZE == head, skip_ref[head], skip)
    step = jnp.concatenate([step_ref[...], step_ref[...]], axis=0)
    log_decay = -step * rate
    parts = []
    for group in range(2):
        v = log_decay[:, group * GROUP : (group + 1) * GROUP]
        first = v.astype(BF16).astype(F32)
        second = (v - first).astype(BF16).astype(F32)
        parts += [first, second, v - first - second]
    upper = (iota((GROUP, GROUP), 0) <= iota((GROUP, GROUP), 1)).astype(F32).astype(BF16)
    sums = dot(jnp.concatenate(parts, axis=0).astype(BF16), upper)
    cum = [sums[g * 24 : g * 24 + 8] + sums[g * 24 + 8 : g * 24 + 16] + sums[g * 24 + 16 : g * 24 + 24] for g in range(2)]
    total_0, total_1 = (jnp.broadcast_to(c[:, GROUP - 1 :], (8, 128)) for c in cum)
    total = total_0 + total_1
    tot[x] = total
    both = jnp.concatenate(cum, axis=1)
    grow = jnp.exp(-both) * step
    decay = jnp.exp(both)
    far_decay = jnp.exp(jnp.concatenate([cum[0], cum[1] + cum[0][:, GROUP - 1 :]], axis=1))
    expander = (iota((8, 256), 0) % 4 == iota((8, 256), 1) // P_SIZE).astype(F32).astype(BF16)

    def expand(v):
        return dot(split_rows(v).T.astype(BF16), expander)

    loads[0].wait()
    drive[...] = (expand(grow) * x_ref[...].astype(F32)).astype(BF16)

    pl.semaphore_wait(barrier, heads - 1 + X - 1 + rows_y - 1)
    b_copies = [z_copy(0, s, b_ref, b_all.at[mine]) for s in range(heads - 1)]
    c_copies = [z_copy(1, s, c_ref, c_all.at[mine]) for s in range(heads - 1)]
    tot_copies = [x_copy(0, a, tot.at[x], tot.at[x]) for a in range(1, X)]
    for copy in b_copies + tot_copies + c_copies:
        copy.start()

    loads[1].wait()
    for level in range(4 + bits_y):
        mix = jnp.concatenate([mix_ref[level], mix_ref[level]], axis=0)
        factor[level] = expand(mix * (decay if level < 2 else far_decay))
    loads[2].wait()
    gate = gate_ref[...].astype(F32)
    silu[...] = gate / (1.0 + jnp.exp(-gate))

    for copy in tot_copies:
        copy.wait()
    totals = [tot[i] for i in range(X)]
    after = jnp.zeros((8, 128), F32)
    row_weight = [None] * X
    for i in reversed(range(X)):
        row_weight[i] = lanes(jnp.exp(after))
        after = after + totals[i]
    row_tot[y] = after
    row_copies = [y_copy(0, a, row_tot.at[y], row_tot.at[y]) for a in range(1, rows_y)]
    for a in range(1, rows_y):
        pl.when(y + a < rows_y)(row_copies[a - 1].start)
    before = jnp.zeros((8, 128), F32)
    for i in range(X):
        before = before + jnp.where(i < x, totals[i], 0.0)
    row_factor = lanes(jnp.exp(before))
    pair_last = jnp.where(x == 3, totals[2], 0.0)
    pair_weight = [lanes(jnp.exp(totals[1] + pair_last)), lanes(jnp.exp(pair_last))]

    loads[3].wait()
    for copy in b_copies:
        copy.wait_recv()
    state_0 = lanes(jnp.exp(total_0)) * dot(b_all[:, :GROUP], drive[:GROUP])
    state_1 = state_0 + dot(b_all[:, GROUP:], drive[GROUP:])
    state[...] = (lanes(jnp.exp(total_1)) * state_1).astype(BF16)
    near_state[...] = state_0.astype(BF16)
    piece_copies = [
        x_copy(1, a, state.at[pl.ds(pl.multiple_of((x + a) % X * cut, cut), cut)], piece.at[x])
        for a in range(1, X)
    ]
    state_copies = [x_copy(2, a, state, row_state.at[x]) for a in range(1, X)]
    for copy in piece_copies:
        copy.start()
    for a in range(1, X):
        pl.when(x + a < X)(state_copies[a - 1].start)
    own_cut = pl.ds(pl.multiple_of(x * cut, cut), cut)
    piece[x] = state[own_cut, :]

    loads[4].wait()
    for copy in c_copies:
        copy.wait_recv()
    ct_ref[...] = c_all[...].astype(F32).T.astype(BF16)

    for copy in piece_copies:
        copy.wait_recv()
    row = sum(row_weight[i] * piece[i].astype(F32) for i in range(X))
    row_sum[...] = row.astype(BF16)
    sum_copies = [y_copy(1, a, row_sum, row_in.at[y]) for a in range(1, rows_y)]
    for a in range(1, rows_y):
        pl.when(y + a < rows_y)(sum_copies[a - 1].start)

    causal = iota((GROUP, GROUP), 0) >= iota((GROUP, GROUP), 1)
    for group in range(2):
        rows = slice(group * GROUP, (group + 1) * GROUP)
        scores = dot(ct_ref[rows], b_all[:, rows])
        scores = jnp.where(causal, scores, 0.0).astype(BF16)
        acc = factor[0, rows] * dot(scores, drive[rows]) + skip * x_ref[rows].astype(F32)
        if group == 1:
            acc = acc + factor[1, rows] * dot(ct_ref[rows], near_state[...])
        pre[rows] = acc

    for a in range(1, X):
        pl.when(x - a >= 0)(state_copies[a - 1].wait_recv)

    @pl.when(x % 2 == 1)
    def _():
        pre[...] += factor[2] * dot(ct_ref[...], row_state[x - 1])

    @pl.when(x >= 2)
    def _():
        pair = pair_weight[0] * row_state[0].astype(F32) + pair_weight[1] * row_state[1].astype(F32)
        pre[...] += factor[3] * dot(ct_ref[...], pair.astype(BF16))

    for a in range(1, rows_y):
        pl.when(y - a >= 0)(row_copies[a - 1].wait_recv)
    gap = jnp.zeros((8, 128), F32)
    row_gap = [None] * rows_y
    for q in reversed(range(rows_y - 1)):
        row_gap[q] = lanes(jnp.exp(gap))
        gap = gap + jnp.where(q < y, row_tot[q], 0.0)
    for a in range(1, rows_y):
        pl.when(y - a >= 0)(sum_copies[a - 1].wait_recv)
    spans = [jnp.zeros((cut, 256), F32)] * bits_y
    for q in range(rows_y - 1):
        part = row_gap[q] * row_in[q].astype(F32)
        for bit in range(bits_y):
            hit = jnp.logical_and(q // 2 ** (bit + 1) == y // 2 ** (bit + 1), q // 2**bit < y // 2**bit)
            spans[bit] = spans[bit] + jnp.where(hit, part, 0.0)
    span[own_cut] = jnp.concatenate(spans, axis=1).astype(BF16)
    span_copies = [x_copy(3, a, span.at[own_cut], span.at[own_cut]) for a in range(1, X)]
    for copy in span_copies:
        copy.start()
    for copy in span_copies:
        copy.wait()

    ones = jnp.ones((8, 128), BF16)
    far = factor[4] * dot(ct_ref[...], span[:, :256])
    for bit in range(1, bits_y):
        far = far + factor[4 + bit] * dot(ct_ref[...], span[:, bit * 256 : (bit + 1) * 256])
    g = (pre[...] + row_factor * far) * silu[...]
    gg = g * g
    gg = gg[:, :128] + gg[:, 128:]
    high = gg.astype(BF16)
    low = (gg - high.astype(F32)).astype(BF16)
    flat = (((1,), (1,)), ((), ()))
    line = lax.dot_general(ones, high, flat, preferred_element_type=F32)
    line = line + lax.dot_general(ones, low, flat, preferred_element_type=F32)
    packed = jnp.concatenate([line[0:1, j * 128 : (j + 1) * 128] for j in range(4)], axis=0)
    squares[col] = packed
    square_copies = [z_copy(2, s, squares.at[col], squares.at[col]) for s in range(heads - 1)]
    for copy in square_copies:
        copy.start()
    gated[...] = g * gain_ref[...]

    for copy in b_copies + c_copies:
        copy.wait_send()
    for copy in piece_copies:
        copy.wait_send()
    for a in range(1, X):
        pl.when(x + a < X)(state_copies[a - 1].wait_send)
    for a in range(1, rows_y):
        pl.when(y + a < rows_y)(row_copies[a - 1].wait_send)
        pl.when(y + a < rows_y)(sum_copies[a - 1].wait_send)

    for copy in square_copies:
        copy.wait()
    summed = squares[0]
    for k in range(1, heads):
        summed = summed + squares[k]
    scale = lax.rsqrt(summed / (heads * 256) + EPS)
    scale = jnp.concatenate([jnp.broadcast_to(scale[j : j + 1], (8, 128)) for j in range(4)], axis=1)
    wide = dot((split_rows(scale) * 0.25).T.astype(BF16), ones)
    for half in range(2):
        cols = slice(half * 128, (half + 1) * 128)
        out_ref[:, cols] = (gated[:, cols] * wide).astype(BF16)


def on_device(rows_y, chips_z, inputs, gate, input_map, output_map, step, decay_rate, level_mix, skip, norm_gain):
    tokens, width = inputs.shape
    cut = N // X
    bits_y = rows_y.bit_length() - 1
    heads = 2 * chips_z
    vmem = pl.BlockSpec(memory_space=pltpu.VMEM)
    smem = pl.BlockSpec(memory_space=pltpu.SMEM)
    hbm = pl.BlockSpec(memory_space=pl.ANY)
    scratch = [
        pltpu.VMEM((tokens, width), BF16),
        pltpu.VMEM((tokens, width), BF16),
        pltpu.VMEM(level_mix.shape, F32),
        pltpu.VMEM((N, tokens), BF16),
        pltpu.VMEM((N, tokens), BF16),
        pltpu.VMEM((tokens, width), BF16),
        pltpu.VMEM((4 + bits_y, tokens, width), F32),
        pltpu.VMEM((tokens, width), F32),
        pltpu.VMEM((tokens, width), F32),
        pltpu.VMEM((tokens, width), F32),
        pltpu.VMEM((tokens, N), BF16),
        pltpu.VMEM((N, width), BF16),
        pltpu.VMEM((X, cut, width), BF16),
        pltpu.VMEM((X, N, width), BF16),
        pltpu.VMEM((X, 8, 128), F32),
        pltpu.VMEM((rows_y, 8, 128), F32),
        pltpu.VMEM((cut, width), BF16),
        pltpu.VMEM((rows_y, cut, width), BF16),
        pltpu.VMEM((N, bits_y * width), BF16),
        pltpu.VMEM((heads, 4, 128), F32),
        pltpu.VMEM((N, width), BF16),
        pltpu.SemaphoreType.DMA((5,)),
        pltpu.SemaphoreType.DMA((3, heads - 1)),
        pltpu.SemaphoreType.DMA((3, heads - 1)),
        pltpu.SemaphoreType.DMA((4, X)),
        pltpu.SemaphoreType.DMA((4, X)),
        pltpu.SemaphoreType.DMA((2, rows_y)),
        pltpu.SemaphoreType.DMA((2, rows_y)),
    ]
    return pl.pallas_call(
        functools.partial(kernel, rows_y, chips_z),
        out_shape=jax.ShapeDtypeStruct((tokens, width), BF16),
        in_specs=[hbm, hbm, vmem, vmem, vmem, smem, hbm, smem, vmem],
        out_specs=vmem,
        scratch_shapes=scratch,
        compiler_params=pltpu.CompilerParams(collective_id=0, has_side_effects=True),
    )(inputs, gate, input_map, output_map, step, decay_rate, level_mix, skip, norm_gain.reshape(1, width))


def solution(mesh):
    rows_y, chips_z = mesh.shape["seq"] // X, mesh.shape["head"] // 2
    return jax.shard_map(
        functools.partial(on_device, rows_y, chips_z),
        mesh=mesh,
        in_specs=(
            P("seq", "head"),
            P("seq", "head"),
            P("head", "seq"),
            P("head", "seq"),
            P("head", "seq"),
            P("head"),
            P(None, "head", "seq"),
            P("head"),
            P("head"),
        ),
        out_specs=P("seq", "head"),
        check_vma=False,
    )
```
